32 devices in a mesh: dp: 16 (over z, x, core), expert: 2 (over y).
Axes of the slice: x: 2, y: 2, z: 4, core: 2. Of those that a mesh axis runs over, the one named last changes fastest.
Arguments:
- tokens: bfloat16 [2048, 2048], P('dp', 'expert'), may hold values from -6 to 6
- gate_probs: float32 [2048, 6], P('dp'), may hold values from 0.05 to 0.4
- routes: int32 [2048, 6], P('dp'), may hold values from 0 to 15, all different within a row; in each aligned block of 128 rows (0 to 127, 128 to 255, ...) at most 54 rows name the same one
- gate_weight: bfloat16 [16, 1408, 2048], P('dp', 'expert'), may hold values from -0.125 to 0.125
- up_weight: bfloat16 [16, 1408, 2048], P('dp', 'expert'), may hold values from -0.125 to 0.125
- down_weight: bfloat16 [16, 1408, 2048], P('dp', 'expert'), may hold values from -0.15625 to 0.15625
- out_grad: bfloat16 [2048, 2048], P('dp', 'expert'), may hold values from -6 to 6
Outputs:
- layer_out: bfloat16 [2048, 2048], P('dp', 'expert')
- d_tokens: bfloat16 [2048, 2048], P('dp', 'expert')
- gate_grad: float32 [2048, 6], P('dp')
- d_gate_weight: bfloat16 [16, 1408, 2048], P('dp', 'expert')
- d_up_weight: bfloat16 [16, 1408, 2048], P('dp', 'expert')
- d_down_weight: bfloat16 [16, 1408, 2048], P('dp', 'expert')
The draws below stay inside these ranges and needn't reach their ends.
Inputs may be any that keep to these rules, and one draw needn't show every extreme that they name: `routes`: each row names 6 different experts. In every aligned block of 128 rows no expert is named by more than 54 rows, a bound that some block reaches.
All inputs are finite; a program needn't handle non-finite values.
Results may differ from the reference program's by a relative error of at most 0.0085.
Values may be sent and summed in bfloat16 or wider, within the bound.
No kernel may reach another device: no remote copies, remote signals or barrier semaphores. Data moves between devices by JAX's collectives and lax.ppermute only.
A program may use at most 128 MiB of HBM per device.

```python
import math
import jax
import jax.numpy as jnp
import numpy as np
from jax import lax

D = 2048
FF = 1408
TOP = 6
TOK_DEV = 128
EXPERTS = 16
TOKENS = 2048
CAP = 54
HS = 704
N_DP = 16


def block_scale(stream_key, dims, cuts, smallest, top_value):
    gain = 1.0
    for axis_at, shards_of in cuts:
        draws = jax.random.uniform(jax.random.fold_in(jax.random.fold_in(stream_key, 6), axis_at), (shards_of,), jnp.float32, smallest / len(cuts), top_value / len(cuts))
        gain = gain * jnp.repeat(jnp.exp(draws), dims[axis_at] // shards_of).reshape((-1,) + (1,) * (len(dims) - 1 - axis_at))
    return gain


def deal_out(key, own, number, rows, count, top, reach, slope):
    order = jax.random.permutation(key, count)
    heavy_load, ordinary = portions_of(count, rows * top, reach, slope, True), portions_of(count, rows * top, reach, slope, False)
    places = jnp.arange(count)

    def named(lengths, rotation):
        used = int((lengths > 0).sum())
        fixed = max(1, used // 4)
        shifted = fixed + (places - fixed + rotation * (used - fixed)) % max(1, count - fixed)
        return jnp.zeros((count,), jnp.int32).at[order[jnp.where(places < fixed, places, shifted)]].set(jnp.asarray(lengths, jnp.int32))

    lengths = jnp.where(number % 4 == 0, named(heavy_load, number // 4), named(ordinary, number - number // 4 - 1))
    mixed = jax.random.permutation(jax.random.fold_in(own, 3), count)
    source_of, receiver = mixed[0:count // 2 * 2:2], mixed[1:count // 2 * 2:2]
    slack = jnp.minimum(lengths[source_of] - 1, reach - lengths[receiver]) // 2
    slack = jnp.where((source_of == order[0]) | (receiver == order[0]) | (lengths[receiver] == 0), 0, jnp.maximum(slack, 0))
    shifted = jax.random.randint(jax.random.fold_in(own, 4), (count // 2,), 0, 1 << 20) % (slack + 1)
    lengths = lengths.at[source_of].add(-shifted).at[receiver].add(shifted)
    members = jnp.searchsorted(jnp.cumsum(lengths), jnp.arange(rows * top), side="right").astype(jnp.int32)
    table = members.reshape(top, rows).T
    table = table[jax.random.permutation(jax.random.fold_in(own, 1), rows)]
    rotation = jax.random.randint(jax.random.fold_in(own, 2), (rows, 1), 0, top)
    return jnp.take_along_axis(table, (jnp.arange(top)[None, :] + rotation) % top, axis=1)


def portions_of(count, total, reach, lean, full):
    loads = [(1 << 20) // math.isqrt(rank ** lean) + 1 for rank in range(1, count + 1)]
    largest = reach if full else min(reach, max(-(-total // count), total * loads[0] // sum(loads)))
    least = 1 if total - largest >= count - 1 else 0
    holding, surplus = [largest] + [least] * (count - 1), total - largest - least * (count - 1)
    while surplus > 0:
        free = [i for i in range(1, count) if holding[i] < largest] or [i for i in range(1, count) if holding[i] < reach]
        mass, left = sum([loads[i] for i in free]), surplus
        for i in free:
            extra = min(reach - holding[i], max(1, left * loads[i] // mass), surplus)
            holding[i] = holding[i] + extra
            surplus = surplus - extra
    return np.array(holding)


def scatter_about(key, dims, width, most, split=(), kind=jnp.bfloat16):
    loudness = block_scale(key, dims, split, -0.22, 0.18) if split else 1.0
    values = jax.random.normal(key, dims, jnp.float32) * width * loudness
    return jnp.minimum(jnp.maximum(values, -most), most).astype(kind)


def setup_inputs(seed: int = 0) -> dict:
    streams_of = jax.random.split(jax.random.key(seed), 8)
    tokens = scatter_about(streams_of[0], (TOKENS, D), 1.0, 6.0, ((0, 16), (1, 2)))
    gate_probs = jnp.clip(0.05 + 0.35 * jax.random.uniform(streams_of[1], (TOKENS, TOP), jnp.float32) ** block_scale(streams_of[1], (TOKENS, TOP), ((0, 16),), -0.2, 0.2), 0.05, 0.4)
    routes_keys = jax.random.split(jax.random.fold_in(streams_of[2], 1), TOKENS // TOK_DEV)
    routes_turns = jax.random.permutation(jax.random.fold_in(streams_of[2], 3), TOKENS // TOK_DEV)
    routes = jax.vmap(lambda own, number: deal_out(jax.random.fold_in(streams_of[2], 2), own, number, TOK_DEV, EXPERTS, TOP, CAP, 2))(routes_keys, routes_turns).reshape((TOKENS, TOP))
    gate_weight = scatter_about(streams_of[3], (EXPERTS, FF, D), D ** -0.5, 0.125, ((0, 16), (1, 2)))
    up_weight = scatter_about(streams_of[4], (EXPERTS, FF, D), D ** -0.5, 0.125, ((0, 16), (1, 2)))
    down_weight = scatter_about(streams_of[5], (EXPERTS, FF, D), FF ** -0.5, 0.15625, ((0, 16), (1, 2)))
    out_grad = scatter_about(streams_of[6], (TOKENS, D), 1.0, 6.0, ((0, 16), (1, 2)))
    return {"tokens": tokens, "gate_probs": gate_probs, "routes": routes, "gate_weight": gate_weight, "up_weight": up_weight, "down_weight": down_weight, "out_grad": out_grad}


def reference(tokens, gate_probs, routes, gate_weight, up_weight, down_weight, out_grad):
    slots_all = N_DP * CAP
    flat_routes = routes.reshape(N_DP, TOK_DEV * TOP)
    onehot = (flat_routes[:, :, None] == jnp.arange(EXPERTS, dtype=jnp.int32)[None, None, :]).astype(jnp.int32)
    earlier = jnp.cumsum(onehot, axis=1) - onehot
    slot_index = jnp.sum(earlier * onehot, axis=2)
    source = jnp.arange(N_DP, dtype=jnp.int32)[:, None]
    target = (flat_routes * slots_all + source * CAP + slot_index).reshape(-1).astype(jnp.int32)
    token_index = jnp.repeat(jnp.arange(TOKENS, dtype=jnp.int32), TOP)
    table = jnp.full((EXPERTS * slots_all,), TOKENS, jnp.int32).at[target].set(token_index).reshape(EXPERTS, slots_all)
    slot_gate = jnp.zeros((EXPERTS * slots_all,), jnp.float32).at[target].set(gate_probs.reshape(-1)).reshape(EXPERTS, slots_all)
    padded_tokens = jnp.concatenate([tokens, jnp.zeros((1, D), tokens.dtype)], axis=0)
    padded_grad = jnp.concatenate([out_grad, jnp.zeros((1, D), out_grad.dtype)], axis=0)
    block_count = FF // HS

    def block_sum(left, right):
        blocks = jnp.einsum("rbh,bhd->rbd", left.astype(jnp.float32).reshape(slots_all, block_count, HS),
                            right.astype(jnp.float32).reshape(block_count, HS, D))
        rounded = lax.optimization_barrier(blocks.astype(jnp.bfloat16))
        return jnp.sum(rounded.astype(jnp.float32), axis=1)

    def per_expert(carry, expert_in):
        out_acc, grad_acc = carry
        w_gate, w_up, w_down, rows_table, gates_here = expert_in
        inputs = padded_tokens[rows_table]
        cot_rows = padded_grad[rows_table]
        grads_in = (gates_here[:, None] * cot_rows.astype(jnp.float32)).astype(jnp.bfloat16)
        pre_gate = jnp.dot(inputs, w_gate.T, preferred_element_type=jnp.float32)
        pre_up = jnp.dot(inputs, w_up.T, preferred_element_type=jnp.float32)
        sigmoid_gate = jax.nn.sigmoid(pre_gate)
        activated = pre_gate * sigmoid_gate
        hidden = (activated * pre_up).astype(jnp.bfloat16)
        expert_out = block_sum(hidden, w_down)
        gate_slots = jnp.sum(cot_rows.astype(jnp.float32) * expert_out, axis=1)
        out_acc = out_acc.at[rows_table].add(gates_here[:, None] * expert_out)
        d_hidden = jnp.dot(grads_in, w_down.T, preferred_element_type=jnp.float32)
        d_down = jnp.dot(hidden.T, grads_in, preferred_element_type=jnp.float32).astype(jnp.bfloat16)
        d_pre_gate = (d_hidden * pre_up * sigmoid_gate * (1.0 + pre_gate * (1.0 - sigmoid_gate))).astype(jnp.bfloat16)
        d_pre_up = (d_hidden * activated).astype(jnp.bfloat16)
        d_gate_w = jnp.dot(d_pre_gate.T, inputs, preferred_element_type=jnp.float32).astype(jnp.bfloat16)
        d_up_w = jnp.dot(d_pre_up.T, inputs, preferred_element_type=jnp.float32).astype(jnp.bfloat16)
        blocks_g = jnp.einsum("rbh,bhd->rbd", d_pre_gate.astype(jnp.float32).reshape(slots_all, block_count, HS),
                              w_gate.astype(jnp.float32).reshape(block_count, HS, D))
        blocks_u = jnp.einsum("rbh,bhd->rbd", d_pre_up.astype(jnp.float32).reshape(slots_all, block_count, HS),
                              w_up.astype(jnp.float32).reshape(block_count, HS, D))
        rounded = lax.optimization_barrier((blocks_g + blocks_u).astype(jnp.bfloat16))
        grad_out = jnp.sum(rounded.astype(jnp.float32), axis=1)
        grad_acc = grad_acc.at[rows_table].add(grad_out)
        return (out_acc, grad_acc), (gate_slots, d_gate_w, d_up_w, d_down)

    start = (jnp.zeros((TOKENS + 1, D), jnp.float32), jnp.zeros((TOKENS + 1, D), jnp.float32))
    (out_acc, grad_acc), (gate_slots, d_gate_weight, d_up_weight, d_down_weight) = lax.scan(
        per_expert, start, (gate_weight, up_weight, down_weight, table, slot_gate))
    layer_out = out_acc[:TOKENS].astype(jnp.bfloat16)
    d_tokens = grad_acc[:TOKENS].astype(jnp.bfloat16)
    gate_grad = gate_slots.reshape(-1)[target].reshape(TOKENS, TOP)
    return (layer_out, d_tokens, gate_grad, d_gate_weight, d_up_weight, d_down_weight)
```

```python
import functools

import jax
import jax.numpy as jnp
from jax import lax
from jax.experimental import pallas as pl
from jax.experimental.pallas import tpu as pltpu
from jax.sharding import PartitionSpec as P

QUAD = 4


def split3(value):
    high = value.astype(jnp.bfloat16)
    rest = value - high.astype(jnp.float32)
    middle = rest.astype(jnp.bfloat16)
    low = (rest - middle.astype(jnp.float32)).astype(jnp.bfloat16)
    return high, middle, low


def vmem(count):
    return [pl.BlockSpec(memory_space=pltpu.VMEM)] * count


def params():
    return pltpu.CompilerParams(vmem_limit_bytes=48 * 1024 * 1024)


def prep_kernel(index_ref, routes_ref, probs_ref, tokens_ref, out_ref):
    rows, width = tokens_ref.shape
    experts = out_ref.shape[0] - rows
    me = index_ref[0]
    routes = routes_ref[...]
    probs = probs_ref[...]
    count = index_ref.shape[0] - 1
    dense = [
        jnp.sum(jnp.where(routes == (me ^ k), probs, 0.0), axis=0, keepdims=True)
        for k in range(count)
    ]
    per_row = width // rows
    wide = [
        jnp.concatenate(dense[k : k + per_row], axis=1) for k in range(0, count, per_row)
    ]
    stacked = jnp.concatenate(wide, axis=0)
    parts = split3(stacked)
    used = 3 * len(wide)
    extra = jnp.concatenate(
        [p.astype(jnp.float32) for p in parts]
        + [jnp.zeros((experts - used, width), jnp.float32)],
        axis=0,
    )
    out_ref[0:rows, :] = tokens_ref[...]
    out_ref[rows:, :] = extra.astype(jnp.bfloat16)


def one_hot(weights, slots, i, cap, nz):
    rows = weights.shape[1]
    total = nz * cap
    line = lax.broadcasted_iota(jnp.int32, (total, rows), 0).astype(jnp.float32)
    pieces = []
    for j in range(nz):
        k = j * QUAD + i
        pieces.append(jnp.where(line == slots[k : k + 1, :] + float(j * cap), 1.0, 0.0))
    return jnp.concatenate(pieces, axis=1)


def select_first_kernel(cap, nz, *refs):
    blocks, outs, w_out, s_out = refs[:nz], refs[nz : nz + QUAD], refs[-2], refs[-1]
    rows = w_out.shape[1]
    width = blocks[0].shape[1]
    count = nz * QUAD
    per_row = width // rows
    lines = count // per_row
    found = []
    for j in range(nz):
        extra = blocks[j][rows:, :].astype(jnp.float32)
        for i in range(QUAD):
            k = j * QUAD + i
            at, col = k // per_row, (k % per_row) * rows
            part = [extra[at + m * lines : at + m * lines + 1, col : col + rows] for m in range(3)]
            found.append(part[0] + part[1] + part[2])
    weights = jnp.concatenate(found, axis=0)
    hit = weights > 0.0
    tri = jnp.where(
        lax.broadcasted_iota(jnp.int32, (rows, rows), 0)
        < lax.broadcasted_iota(jnp.int32, (rows, rows), 1),
        1.0,
        0.0,
    ).astype(jnp.bfloat16)
    before = jnp.dot(
        jnp.where(hit, 1.0, 0.0).astype(jnp.bfloat16), tri, preferred_element_type=jnp.float32
    )
    slots = jnp.where(hit, before, -1e6)
    w_out[...] = weights
    s_out[...] = slots
    data = jnp.concatenate([b[0:rows, :] for b in blocks], axis=0)
    for i in range(QUAD):
        pick = one_hot(weights, slots, i, cap, nz).astype(jnp.bfloat16)
        outs[i][...] = jnp.dot(pick, data, preferred_element_type=jnp.float32).astype(jnp.bfloat16)


def select_scaled_kernel(cap, nz, w_ref, s_ref, *refs):
    blocks, outs = refs[:nz], refs[nz:]
    weights, slots = w_ref[...], s_ref[...]
    data = jnp.concatenate([b[...] for b in blocks], axis=0)
    for i in range(QUAD):
        pick = one_hot(weights, slots, i, cap, nz)
        wide = jnp.concatenate(
            [weights[j * QUAD + i : j * QUAD + i + 1, :] for j in range(nz)], axis=1
        )
        scale = jnp.sum(pick * wide, axis=1, keepdims=True)
        picked = jnp.dot(pick.astype(jnp.bfloat16), data, preferred_element_type=jnp.float32)
        outs[i][...] = (scale * picked).astype(jnp.bfloat16)


def combine_kernel(cap, nz, weighted, w_ref, s_ref, *refs):
    pieces, outs = refs[:QUAD], refs[QUAD:]
    weights, slots = w_ref[...], s_ref[...]
    rows = weights.shape[1]
    total = None

    def turned(pick, data):
        return lax.dot_general(
            pick, data, (((0,), (0,)), ((), ())), preferred_element_type=jnp.float32
        )

    for i in range(QUAD):
        pick = one_hot(weights, slots, i, cap, nz)
        data = pieces[i][...]
        if weighted:
            wide = jnp.concatenate(
                [weights[j * QUAD + i : j * QUAD + i + 1, :] for j in range(nz)], axis=1
            )
            scaled = pick * wide
            high = scaled.astype(jnp.bfloat16)
            low = (scaled - high.astype(jnp.float32)).astype(jnp.bfloat16)
            part = turned(high, data) + turned(low, data)
        else:
            part = turned(pick.astype(jnp.bfloat16), data)
        total = part if total is None else total + part
    for j in range(nz):
        outs[j][...] = total[j * rows : (j + 1) * rows, :].astype(jnp.bfloat16)


def contract_rows(left, right):
    return lax.dot_general(
        left, right, (((0,), (0,)), ((), ())), preferred_element_type=jnp.float32
    )


def contract_last(left, right):
    return lax.dot_general(
        left, right, (((1,), (1,)), ((), ())), preferred_element_type=jnp.float32
    )


def fast(tokens, gate_probs, routes, gate_weight, up_weight, down_weight, out_grad):
    rows, width = tokens.shape
    top = routes.shape[1]
    n_dp = lax.axis_size("dp")
    nz = n_dp // QUAD
    cap = rows * top * 9 // (8 * n_dp)
    slots_q = nz * cap
    slots_all = n_dp * cap
    me = lax.axis_index("dp")
    side = lax.axis_index("expert")
    hidden_count = gate_weight.shape[1]

    def hop(value, k):
        return lax.ppermute(value, "dp", [(s, s ^ k) for s in range(n_dp)])

    def swap(value):
        return lax.ppermute(value, "expert", [(0, 1), (1, 0)])

    bf = functools.partial(jax.ShapeDtypeStruct, dtype=jnp.bfloat16)
    f32 = functools.partial(jax.ShapeDtypeStruct, dtype=jnp.float32)

    lines = 3 * n_dp * rows // width
    extra_rows = -(-lines // 8) * 8
    index = jnp.broadcast_to(me, (n_dp + 1,)).astype(jnp.int32)
    extended = pl.pallas_call(
        prep_kernel,
        out_shape=bf((rows + extra_rows, width)),
        in_specs=[pl.BlockSpec(memory_space=pltpu.SMEM)] + vmem(3),
        out_specs=pl.BlockSpec(memory_space=pltpu.VMEM),
        name="prep",
    )(index, routes.T, gate_probs.T, tokens)
    x_blocks = [extended] + [hop(extended, QUAD * j) for j in range(1, nz)]
    g_blocks = [out_grad] + [hop(out_grad, QUAD * j) for j in range(1, nz)]
    *x_rows, weights, slots = pl.pallas_call(
        functools.partial(select_first_kernel, cap, nz),
        out_shape=[bf((slots_q, width))] * QUAD + [f32((n_dp, rows))] * 2,
        in_specs=vmem(nz),
        out_specs=vmem(QUAD + 2),
        compiler_params=params(),
        name="select_x",
    )(*x_blocks)
    g_rows = pl.pallas_call(
        functools.partial(select_scaled_kernel, cap, nz),
        out_shape=[bf((slots_q, width))] * QUAD,
        in_specs=vmem(nz + 2),
        out_specs=vmem(QUAD),
        compiler_params=params(),
        name="select_g",
    )(weights, slots, *g_blocks)

    def gather(pieces):
        mine = [pieces[0]] + [hop(pieces[i], i) for i in range(1, QUAD)]
        theirs = [swap(piece) for piece in mine]
        mine, theirs = jnp.concatenate(mine, axis=0), jnp.concatenate(theirs, axis=0)
        return jnp.concatenate(
            [jnp.where(side == 0, mine, theirs), jnp.where(side == 0, theirs, mine)], axis=1
        )

    inputs = gather(x_rows)
    grads_in = gather(g_rows)
    w_gate, w_up, w_down = gate_weight[0], up_weight[0], down_weight[0]

    def halves(weight):
        other = lax.dynamic_slice_in_dim(weight, (1 - side) * width, width, axis=1)
        own = lax.dynamic_slice_in_dim(weight, side * width, width, axis=1)
        return other, own

    def give_back(left, weight):
        other, own = halves(weight)
        far = jnp.dot(left, other, preferred_element_type=jnp.float32).astype(jnp.bfloat16)
        near = jnp.dot(left, own, preferred_element_type=jnp.float32)
        pieces = [None] * QUAD
        for i in reversed(range(QUAD)):
            at = slice(i * slots_q, (i + 1) * slots_q)
            both = (near[at] + swap(far[at]).astype(jnp.float32)).astype(jnp.bfloat16)
            pieces[i] = both if i == 0 else hop(both, i)
        return pieces

    def combine(pieces, weighted):
        blocks = pl.pallas_call(
            functools.partial(combine_kernel, cap, nz, weighted),
            out_shape=[bf((rows, width))] * nz,
            in_specs=vmem(QUAD + 2),
            out_specs=vmem(nz),
            compiler_params=params(),
            name="combine_out" if weighted else "combine_grad",
        )(weights, slots, *pieces)
        total = blocks[0].astype(jnp.float32)
        for j in range(1, nz):
            total = total + hop(blocks[j], QUAD * j).astype(jnp.float32)
        return total.astype(jnp.bfloat16)

    pre_gate = contract_last(inputs, w_gate)
    pre_up = contract_last(inputs, w_up)
    sigmoid_gate = jax.nn.sigmoid(pre_gate)
    activated = pre_gate * sigmoid_gate
    hidden = (activated * pre_up).astype(jnp.bfloat16)
    layer_out = combine(give_back(hidden, w_down), True)

    d_hidden = contract_last(grads_in, w_down)
    d_pre_gate = (
        d_hidden * pre_up * sigmoid_gate * (1.0 + pre_gate * (1.0 - sigmoid_gate))
    ).astype(jnp.bfloat16)
    d_pre_up = (d_hidden * activated).astype(jnp.bfloat16)
    slot_dot = jnp.sum(activated * pre_up * d_hidden, axis=1).reshape(QUAD, slots_q)
    both_pre = jnp.concatenate([d_pre_gate, d_pre_up], axis=1)
    both_weights = jnp.concatenate([w_gate, w_up], axis=0)
    d_tokens = combine(give_back(both_pre, both_weights), False)
    d_down = contract_rows(hidden, grads_in).astype(jnp.bfloat16)
    d_gate_w = contract_rows(d_pre_gate, inputs).astype(jnp.bfloat16)
    d_up_w = contract_rows(d_pre_up, inputs).astype(jnp.bfloat16)

    slot_dot = slot_dot + swap(slot_dot)
    dots = [slot_dot[0:1]] + [hop(slot_dot[i : i + 1], i) for i in range(1, QUAD)]
    dots = jnp.concatenate(dots, axis=0).reshape(QUAD, nz, cap).transpose(1, 0, 2)
    dots = dots.reshape(n_dp, cap)
    place = jnp.arange(cap, dtype=jnp.float32)[None, :, None] == slots[:, None, :]
    by_token = jnp.sum(jnp.where(place, dots[:, :, None], 0.0), axis=1)
    by_token = by_token.reshape(nz, QUAD, rows)
    scores = [by_token[0]] + [hop(by_token[j], QUAD * j) for j in range(1, nz)]
    scores = jnp.concatenate(scores, axis=0)
    named = routes.T[None, :, :] == (me ^ jnp.arange(n_dp, dtype=jnp.int32))[:, None, None]
    gate_grad = jnp.sum(jnp.where(named, scores[:, None, :], 0.0), axis=0).T / gate_probs
    return layer_out, d_tokens, gate_grad, d_gate_w[None], d_up_w[None], d_down[None]


def on_device(tokens, gate_probs, routes, gate_weight, up_weight, down_weight, out_grad):
    tok_rows = routes.shape[0]
    top_count = routes.shape[1]
    experts_count = lax.axis_size("dp")
    capacity = tok_rows * top_count * 9 // (8 * experts_count)
    slot_total = experts_count * capacity
    feature_count = gate_weight.shape[2]
    slice_count = tokens.shape[1]
    flat_routes = routes.reshape(-1)
    onehot = (flat_routes[:, None] == jnp.arange(experts_count, dtype=jnp.int32)[None, :]).astype(
        jnp.int32
    )
    earlier = jnp.cumsum(onehot, axis=0) - onehot
    slot_index = jnp.sum(earlier * onehot, axis=1)
    target = flat_routes * capacity + slot_index
    matches = target[None, :] == jnp.arange(slot_total, dtype=jnp.int32)[:, None]
    pair_match = matches.reshape(slot_total, tok_rows, top_count).astype(jnp.float32)
    placing_full = jnp.sum(pair_match, axis=2)
    combine = jnp.sum(pair_match * gate_probs[None, :, :], axis=2)
    slot_gate = jnp.sum(combine, axis=1)
    placing = placing_full.astype(jnp.bfloat16)
    whole_grad = lax.all_gather(out_grad, "expert", axis=1, tiled=True)
    send_x = jnp.dot(placing, tokens, preferred_element_type=jnp.float32).astype(jnp.bfloat16)
    send_g = (
        slot_gate[:, None] * jnp.dot(placing, out_grad, preferred_element_type=jnp.float32)
    ).astype(jnp.bfloat16)
    piece_x, piece_g = (
        lax.all_to_all(
            send_x.reshape(experts_count, capacity, slice_count),
            "dp",
            split_axis=0,
            concat_axis=0,
            tiled=True,
        ),
        lax.all_to_all(
            send_g.reshape(experts_count, capacity, slice_count),
            "dp",
            split_axis=0,
            concat_axis=0,
            tiled=True,
        ),
    )
    recv_x, recv_g = (
        lax.all_gather(piece_x, "expert", axis=2, tiled=True),
        lax.all_gather(piece_g, "expert", axis=2, tiled=True),
    )
    inputs = recv_x.reshape(-1, feature_count)
    grads_in = recv_g.reshape(-1, feature_count)
    w_gate = gate_weight[0]
    w_up = up_weight[0]
    w_down = down_weight[0]
    pre_gate = contract_last(inputs, w_gate)
    pre_up = contract_last(inputs, w_up)
    sigmoid_gate = jax.nn.sigmoid(pre_gate)
    activated = pre_gate * sigmoid_gate
    hidden = (activated * pre_up).astype(jnp.bfloat16)
    part_out = jnp.dot(hidden, w_down, preferred_element_type=jnp.float32).astype(jnp.bfloat16)
    part_out = part_out.reshape(experts_count, capacity, feature_count)
    back_out = lax.all_to_all(part_out, "dp", split_axis=0, concat_axis=0, tiled=True)
    d_hidden = contract_last(grads_in, w_down)
    d_down = contract_rows(hidden, grads_in).astype(jnp.bfloat16)
    d_pre_gate = (
        d_hidden * pre_up * sigmoid_gate * (1.0 + pre_gate * (1.0 - sigmoid_gate))
    ).astype(jnp.bfloat16)
    d_pre_up = (d_hidden * activated).astype(jnp.bfloat16)
    d_gate_w = contract_rows(d_pre_gate, inputs).astype(jnp.bfloat16)
    d_up_w = contract_rows(d_pre_up, inputs).astype(jnp.bfloat16)
    both_pre = jnp.concatenate([d_pre_gate, d_pre_up], axis=1)
    both_weights = jnp.concatenate([w_gate, w_up], axis=0)
    part_grad = jnp.dot(both_pre, both_weights, preferred_element_type=jnp.float32).astype(
        jnp.bfloat16
    )
    part_grad = part_grad.reshape(experts_count, capacity, feature_count)
    back_grad = lax.all_to_all(part_grad, "dp", split_axis=0, concat_axis=0, tiled=True)
    out_flat = back_out.reshape(-1, feature_count)
    grad_flat = back_grad.reshape(-1, feature_count)
    gate_high = combine.astype(jnp.bfloat16)
    gate_low = (combine - gate_high.astype(jnp.float32)).astype(jnp.bfloat16)
    mixed_part = contract_rows(gate_high, out_flat) + contract_rows(gate_low, out_flat)
    grad_part = contract_rows(placing, grad_flat)
    pair_scores = contract_last(out_flat, whole_grad)
    slot_dot = jnp.sum(pair_scores * placing_full, axis=1)
    gate_part = slot_dot[target].reshape(tok_rows, top_count)
    layer_sum, token_sum = (
        lax.psum_scatter(mixed_part, "expert", scatter_dimension=1, tiled=True),
        lax.psum_scatter(grad_part, "expert", scatter_dimension=1, tiled=True),
    )
    gate_grad = lax.psum(gate_part, "expert")
    return (
        layer_sum.astype(jnp.bfloat16),
        token_sum.astype(jnp.bfloat16),
        gate_grad,
        d_gate_w[None],
        d_up_w[None],
        d_down[None],
    )


def solution(mesh):
    groups, sides = mesh.shape["dp"], mesh.shape["expert"]
    step = fast if sides == 2 and groups == 16 else on_device
    return jax.shard_map(
        step,
        mesh=mesh,
        in_specs=(
            P("dp", "expert"),
            P("dp", None),
            P("dp", None),
            P("dp", "expert", None),
            P("dp", "expert", None),
            P("dp", "expert", None),
            P("dp", "expert"),
        ),
        out_specs=(
            P("dp", "expert"),
            P("dp", "expert"),
            P("dp", None),
            P("dp", "expert", None),
            P("dp", "expert", None),
            P("dp", "expert", None),
        ),
        check_vma=False,
    )
```
